32 devices in a mesh: grp: 8 (over z, y), blk: 4 (over x, core).
Axes of the slice: x: 2, y: 2, z: 4, core: 2. Of those that a mesh axis runs over, the one named last changes fastest.
Arguments:
- field_phase: float32 [6, 16384], P(None, ('grp', 'blk')), may hold values from -10 to 10
- field_mass: float32 [16384], P(('grp', 'blk')), may hold values from 0.2 to 5
- old_force: float32 [6, 2048], P(None, ('grp', 'blk')), may hold values from -6 to 6
- target_slot: int32 [101, 2048], P(None, ('grp', 'blk')), may hold values from 0 to 12927, as said below
- target_star: int32 [101, 2048], P(None, ('grp', 'blk')), may hold values from 0 to 511
Outputs:
- reg_force: float32 [6, 2048], P(None, ('grp', 'blk'))
- irr_force: float32 [6, 2048], P(None, ('grp', 'blk'))
- new_state: float32 [6, 2048], P(None, ('grp', 'blk'))
The draws below stay inside these ranges and needn't reach their ends.
Inputs may be any that keep to these rules, and one draw needn't show every extreme that they name: `target_slot`: within the 64 columns of one device all slots differ; slot // 404 is the index, grp-major over grp and blk, of the device that holds the star, so at most 404 entries of one device go to one owner, and some owners receive exactly 404 from every device.
All inputs are finite; a program needn't handle non-finite values.
Results may differ from the reference program's by a relative error of at most 0.0003.
Values sent between devices are 32-bit elements; how exact they have to be, the bound alone decides.
No kernel may reach another device: no remote copies, remote signals or barrier semaphores. Data moves between devices by JAX's collectives and lax.ppermute only.
A program may use at most 128 MiB of HBM per device.

```python
import math
import jax
import jax.numpy as jnp
from jax import lax

STAR_DEV = 512
ACT_DEV = 64
NBR = 100
STARS = 16384
ACT = 2048
MOST = 404
HOT = 8
GROUP_STARS = 2048
CLUSTERS = 8
DEVICES = 32


def draw_field_phase(key, part):
    base = jax.random.fold_in(key, 7)
    cluster_of = jnp.arange(STARS, dtype=jnp.int32) // GROUP_STARS
    centres = jax.random.normal(jax.random.fold_in(base, 1), (3, CLUSTERS), jnp.float32)
    spread = 0.8 * jax.random.normal(jax.random.fold_in(base, 2), (3, STARS), jnp.float32)
    velocity = jax.random.normal(jax.random.fold_in(base, 3), (3, STARS), jnp.float32)
    position = jnp.take(centres, cluster_of, axis=1) + spread
    return jnp.clip(jnp.concatenate([position, velocity], axis=0), -10.0, 10.0)


def draw_target_slot(key, part):
    base = jax.random.fold_in(key, 23)
    slot_total = DEVICES * MOST
    owner_rank = jax.random.permutation(jax.random.fold_in(base, 1), DEVICES)
    slot_ids = jnp.arange(slot_total, dtype=jnp.int32)
    owner_of = slot_ids // MOST
    within = slot_ids % MOST
    is_hot = jnp.take(owner_rank, owner_of) < HOT
    allowed = is_hot | (within < MOST // 2)
    target_count = ACT_DEV * (NBR + 1)

    def one_device(device):
        device_key = jax.random.fold_in(base, 1000 + device)
        scores = jax.random.permutation(jax.random.fold_in(device_key, 1), slot_total).astype(jnp.int32)
        priority = jnp.where(is_hot, scores - 2 * slot_total, jnp.where(allowed, scores, scores + 2 * slot_total))
        chosen = jnp.argsort(priority)[:target_count].astype(jnp.int32)
        mixed = jax.random.permutation(jax.random.fold_in(device_key, 2), chosen)
        return mixed.reshape(NBR + 1, ACT_DEV)
    per_device = jax.vmap(one_device)(jnp.arange(DEVICES, dtype=jnp.int32))
    return jnp.transpose(per_device, (1, 0, 2)).reshape(NBR + 1, DEVICES * ACT_DEV).astype(jnp.int32)


def plant(values, own_key, smallest, high):
    longest = values.shape.index(max(values.shape))
    spots = []
    for shift in (0, 1):
        where = [jax.random.randint(jax.random.fold_in(own_key, axis), (), 0, length) for axis, length in enumerate(values.shape)]
        where[longest] = (where[longest] + shift) % values.shape[longest]
        spots.append(tuple(where))
    return values.at[spots[0]].set(smallest).at[spots[1]].set(high)


def shard_levels(key, shape, shards, least, largest):
    loudness, own = 1.0, jax.random.fold_in(key, 6)
    for dim, blocks in shards:
        heights = jnp.exp(jax.random.uniform(jax.random.fold_in(own, dim), (blocks,), jnp.float32, least / len(shards), largest / len(shards)))
        loudness = loudness * jnp.repeat(heights, shape[dim] // blocks).reshape([-1 if axis == dim else 1 for axis in range(len(shape))])
    return loudness


def scatter_about(key, extent, scale, reach, cuts=(), kind=jnp.bfloat16):
    values = jax.random.normal(key, extent, jnp.float32) * scale
    if len(cuts) > 0:
        values = shard_levels(key, extent, cuts, -0.22, 0.18) * values
    return jnp.clip(values, min=-reach, max=reach).astype(kind)


def setup_inputs(seed: int = 0) -> dict:
    keys = jax.random.split(jax.random.key(seed), 6)
    field_phase = draw_field_phase(jax.random.fold_in(keys[5], 71), 0)
    field_mass = jnp.clip(jnp.exp(math.log(5.0) - 3.218876 * jax.random.uniform(keys[1], (STARS,), jnp.float32) ** shard_levels(keys[1], (STARS,), ((0, 32),), -0.2, 0.2)), 0.2, 5.0)
    old_force = scatter_about(keys[2], (6, ACT), 1.0, 6.0, ((1, 32),), jnp.float32)
    target_slot = draw_target_slot(jax.random.fold_in(keys[5], 71), 0)
    target_star = plant(jax.random.randint(keys[4], (NBR + 1, ACT), 0, STAR_DEV), jax.random.fold_in(keys[4], 1), 0, STAR_DEV - 1).astype(jnp.int32)
    return {"field_phase": field_phase, "field_mass": field_mass, "old_force": old_force, "target_slot": target_slot, "target_star": target_star}


soften_sq = 0.01
step_length = 0.5

def pair_block(receivers, emitters):
    separation = emitters[0:3, None, :] - receivers[0:3, :, None]
    rel_velocity = emitters[3:6, None, :] - receivers[3:6, :, None]
    dist_sq = soften_sq + lax.optimization_barrier(jnp.sum(separation * separation, axis=0))
    inverse = lax.rsqrt(dist_sq)
    weight = emitters[6][None, :] * inverse * inverse * inverse
    radial = 3.0 * lax.optimization_barrier(jnp.sum(separation * rel_velocity, axis=0)) / dist_sq
    pull_sum = lax.optimization_barrier(jnp.sum(weight[None] * separation, axis=2))
    jerk_sum = lax.optimization_barrier(jnp.sum(weight[None] * (rel_velocity - radial[None] * separation), axis=2))
    return jnp.concatenate([pull_sum, jerk_sum], axis=0)

def pair_sum(receivers, emitters):
    row_total = receivers.shape[1]
    tile_rows = math.gcd(row_total, 256)
    tiles = receivers.reshape(6, row_total // tile_rows, tile_rows).transpose(1, 0, 2)
    emit_total = emitters.shape[1]
    emit_rows = math.gcd(emit_total, 1024)
    emit_blocks = emitters.reshape(7, emit_total // emit_rows, emit_rows).transpose(1, 0, 2)

    def single_tile(block_rows):

        def add_block(total, emit_piece):
            return (total + pair_block(block_rows, emit_piece), None)
        start = jnp.zeros((6, tile_rows), jnp.float32)
        total, unused = lax.scan(add_block, start, emit_blocks)
        return total
    result = lax.map(single_tile, tiles)
    return result.transpose(1, 0, 2).reshape(6, row_total)

def neighbour_sum(receivers, emitters):
    separation = emitters[0:3] - receivers[0:3, None, :]
    rel_velocity = emitters[3:6] - receivers[3:6, None, :]
    dist_sq = soften_sq + lax.optimization_barrier(jnp.sum(separation * separation, axis=0))
    inverse = lax.rsqrt(dist_sq)
    weight = emitters[6] * inverse * inverse * inverse
    radial = 3.0 * lax.optimization_barrier(jnp.sum(separation * rel_velocity, axis=0)) / dist_sq
    pull_sum = lax.optimization_barrier(jnp.sum(weight[None] * separation, axis=1))
    jerk_sum = lax.optimization_barrier(jnp.sum(weight[None] * (rel_velocity - radial[None] * separation), axis=1))
    return jnp.concatenate([pull_sum, jerk_sum], axis=0)

def corrector(home_state, regular, irregular, old_force):
    accel_new = regular[0:3] + irregular[0:3]
    jerk_new = regular[3:6] + irregular[3:6]
    difference = old_force[0:3] - accel_new
    snap_term = -6.0 * difference - step_length * (4.0 * old_force[3:6] + 2.0 * jerk_new)
    crackle_term = 12.0 * difference + 6.0 * step_length * (old_force[3:6] + jerk_new)
    step_square = step_length * step_length
    position = home_state[0:3] + step_square / 24.0 * snap_term + step_square / 120.0 * crackle_term
    velocity = home_state[3:6] + step_length / 6.0 * snap_term + step_length / 24.0 * crackle_term
    return jnp.concatenate([position, velocity], axis=0)

def reference(field_phase, field_mass, old_force, target_slot, target_star):
    star_table = jnp.concatenate([field_phase, field_mass[None, :]], axis=0)
    global_id = (target_slot // MOST * STAR_DEV + target_star).astype(jnp.int32)
    fetched = jnp.take(star_table, global_id.reshape(-1), axis=1).reshape(7, NBR + 1, ACT)
    own_state = fetched[0:6, 0, :]
    irregular = neighbour_sum(own_state, fetched[:, 1:, :]) / NBR
    regular = pair_sum(own_state, star_table) / STARS
    return (regular, irregular, corrector(own_state, regular, irregular, old_force))
```

```python
import functools

import jax
import jax.numpy as jnp
from jax import lax
from jax.experimental import pallas as pl
from jax.experimental.pallas import tpu as pltpu
from jax.sharding import PartitionSpec as P

soften_sq = 0.01
step_length = 0.5
AXES = ("grp", "blk")
LANES = 128
SUB = 8


def swapped(x, bit, count):
    return lax.ppermute(x, AXES, [(i, i ^ bit) for i in range(count)])


def force_kernel(bits, bucket, active, nbr, local, star_total,
                 me_ref, slot_ref, star_ref, old_ref, near_ref, far_ref,
                 reg_ref, irr_ref, new_ref,
                 slots, stars, found, home, totals):
    entries = nbr + 1
    half = slots.shape[0]
    tiles = local // LANES
    held = near_ref.shape[0]
    groups = active // SUB
    blocks = half // SUB
    me = me_ref[0]

    slots[...] = jnp.full(slots.shape, -1, jnp.int32)
    stars[...] = jnp.zeros(stars.shape, jnp.int32)
    slots[:, 0:active] = slot_ref[0:half, :]
    stars[:, 0:active] = star_ref[0:half, :]
    slots[0:entries - half, active:2 * active] = slot_ref[half:entries, :]
    stars[0:entries - half, active:2 * active] = star_ref[half:entries, :]

    def places(slot, star):
        owner = jnp.floor((slot.astype(jnp.float32) + 0.5) * (1.0 / bucket)).astype(jnp.int32)
        rel = lax.bitwise_xor(owner, me)
        pos = jnp.zeros_like(rel)
        for weight, bit in enumerate(bits):
            shift = bit.bit_length() - 1
            pos = pos + (((rel >> shift) & 1) << weight)
        row = pos * tiles + (star >> 7)
        return jnp.where(slot < 0, -1, row), star & (LANES - 1)

    own_slot = jnp.concatenate([slot_ref[0:1, :], slot_ref[0:1, :]], axis=1)
    own_star = jnp.concatenate([star_ref[0:1, :], star_ref[0:1, :]], axis=1)
    own_row, own_lane = places(own_slot, own_star)
    own_row = jnp.broadcast_to(own_row, (SUB, LANES))
    own_lane = jnp.broadcast_to(own_lane, (SUB, LANES))

    def own_step(ref, base):
        def step(p, own):
            for t in range(tiles):
                data = ref[p, :, t * LANES:(t + 1) * LANES]
                got = jnp.take_along_axis(data, own_lane, axis=1)
                own = jnp.where(own_row == base + p * tiles + t, got, own)
            return own
        return step

    own = jnp.zeros((SUB, LANES), jnp.float32)
    own = lax.fori_loop(0, held, own_step(near_ref, 0), own)
    own = lax.fori_loop(0, held, own_step(far_ref, held * tiles), own)
    turned = own.T
    for c in range(6):
        home[c] = jnp.broadcast_to(turned[0:active, c:c + 1], (active, LANES))

    for b in range(blocks):
        rows = slice(b * SUB, (b + 1) * SUB)
        row, lane = places(slots[rows, :], stars[rows, :])
        slots[rows, :] = row
        stars[rows, :] = lane

    def pair(xi, xj):
        d = [xj[c] - xi[c] for c in range(3)]
        w = [xj[c + 3] - xi[c + 3] for c in range(3)]
        dist_sq = soften_sq + (d[0] * d[0] + d[1] * d[1] + d[2] * d[2])
        inverse = lax.rsqrt(dist_sq)
        inv_sq = inverse * inverse
        weight = xj[6] * inverse * inv_sq
        radial = 3.0 * (d[0] * w[0] + d[1] * w[1] + d[2] * w[2]) * inv_sq
        pull = [weight * d[c] for c in range(3)]
        jerk = [weight * (w[c] - radial * d[c]) for c in range(3)]
        return pull + jerk

    zero = jnp.zeros((SUB, LANES), jnp.float32)
    for g in range(max(groups, blocks)):
        rows = slice(g * SUB, (g + 1) * SUB)
        xi = [home[c, rows, :] for c in range(6)] if g < groups else None
        if g < blocks:
            row, lane = slots[rows, :], stars[rows, :]

        def sweep(ref, base):
            def step(p, carry):
                sums, seen = carry
                for t in range(tiles):
                    xj = [jnp.broadcast_to(ref[p, c:c + 1, t * LANES:(t + 1) * LANES], (SUB, LANES)) for c in range(7)]
                    if g < groups:
                        sums = [s + v for s, v in zip(sums, pair(xi, xj))]
                    if g < blocks:
                        hit = row == base + p * tiles + t
                        seen = [jnp.where(hit, jnp.take_along_axis(x, lane, axis=1), s) for x, s in zip(xj, seen)]
                return sums, seen
            return step

        carry = ([zero] * (6 if g < groups else 0), [zero] * (7 if g < blocks else 0))
        carry = lax.fori_loop(0, held, sweep(near_ref, 0), carry)
        sums, seen = lax.fori_loop(0, held, sweep(far_ref, held * tiles), carry)
        if g < groups:
            for c in range(6):
                totals[c, rows, :] = sums[c]
        if g < blocks:
            for c in range(7):
                found[c, rows, :] = seen[c]

    regular = [jnp.sum(totals[c].T, axis=0, keepdims=True) * (1.0 / star_total) for c in range(6)]
    own_rows = [jnp.broadcast_to(own[c:c + 1, :], (SUB, LANES)) for c in range(6)]
    near = [zero] * 6
    for b in range(blocks):
        rows = slice(b * SUB, (b + 1) * SUB)
        near = [s + v for s, v in zip(near, pair(own_rows, [found[c, rows, :] for c in range(7)]))]
    near = [jnp.sum(v, axis=0, keepdims=True) for v in near]
    irregular = [(v[:, 0:active] + v[:, active:2 * active]) * (1.0 / nbr) for v in near]
    for c in range(6):
        reg_ref[c:c + 1, :] = regular[c]
        irr_ref[c:c + 1, :] = irregular[c]
    for c in range(3):
        accel = regular[c] + irregular[c]
        jerk = regular[c + 3] + irregular[c + 3]
        a0, j0 = old_ref[c:c + 1, :], old_ref[c + 3:c + 4, :]
        difference = a0 - accel
        snap = -6.0 * difference - step_length * (4.0 * j0 + 2.0 * jerk)
        crackle = 12.0 * difference + 6.0 * step_length * (j0 + jerk)
        square = step_length * step_length
        new_ref[c:c + 1, :] = own[c:c + 1, 0:active] + square / 24.0 * snap + square / 120.0 * crackle
        new_ref[c + 3:c + 4, :] = own[c + 3:c + 4, 0:active] + step_length / 6.0 * snap + step_length / 24.0 * crackle


def per_device(field_phase, field_mass, old_force, target_slot, target_star):
    entries, active = target_slot.shape
    count = lax.axis_size("grp") * lax.axis_size("blk")
    local = field_phase.shape[1]
    nbr = entries - 1
    bucket = 2 * ((entries * active + count - 1) // count)
    assert count & (count - 1) == 0 and 2 * active == LANES and local % LANES == 0
    half = -(-((entries + 1) // 2) // SUB) * SUB
    me = lax.axis_index("grp") * lax.axis_size("blk") + lax.axis_index("blk")
    bits = [1 << b for b in reversed(range(count.bit_length() - 1))]
    table = jnp.concatenate([field_phase, field_mass[None, :], jnp.zeros((1, local), jnp.float32)], axis=0)[None]
    for bit in bits[:-1]:
        table = jnp.concatenate([table, swapped(table, bit, count)], axis=0)
    other = swapped(table, bits[-1], count)
    vmem = pl.BlockSpec(memory_space=pltpu.VMEM)
    out = jax.ShapeDtypeStruct((6, active), jnp.float32)
    return pl.pallas_call(
        functools.partial(force_kernel, bits, bucket, active, nbr, local, local * count),
        out_shape=(out, out, out),
        in_specs=[pl.BlockSpec(memory_space=pltpu.SMEM)] + [vmem] * 5,
        out_specs=(vmem, vmem, vmem),
        scratch_shapes=[
            pltpu.VMEM((half, LANES), jnp.int32),
            pltpu.VMEM((half, LANES), jnp.int32),
            pltpu.VMEM((7, half, LANES), jnp.float32),
            pltpu.VMEM((6, active, LANES), jnp.float32),
            pltpu.VMEM((6, active, LANES), jnp.float32),
        ],
        name="forces",
    )(me.astype(jnp.int32).reshape(1), target_slot, target_star, old_force, table, other)


def solution(mesh):
    spec = P(None, AXES)
    return jax.shard_map(
        per_device, mesh=mesh, in_specs=(spec, P(AXES), spec, spec, spec),
        out_specs=(spec, spec, spec), check_vma=False,
    )
```

```python
import functools

import jax
import jax.numpy as jnp
from jax import lax
from jax.experimental import pallas as pl
from jax.experimental.pallas import tpu as pltpu
from jax.sharding import PartitionSpec as P

soften_sq = 0.01
step_length = 0.5
AXES = ("grp", "blk")
LANES = 128
SUB = 8
BLOCK = LANES // SUB


def swapped(x, bit, count):
    return lax.ppermute(x, AXES, [(i, i ^ bit) for i in range(count)])


def pair(xi, xj):
    d = [xj[c] - xi[c] for c in range(3)]
    w = [xj[c + 3] - xi[c + 3] for c in range(3)]
    dist_sq = soften_sq + (d[0] * d[0] + d[1] * d[1] + d[2] * d[2])
    inverse = lax.rsqrt(dist_sq)
    inv_sq = inverse * inverse
    weight = (xj[6] * inverse) * inv_sq
    radial = (d[0] * w[0] + d[1] * w[1] + d[2] * w[2]) * inv_sq
    pull = [weight * d[c] for c in range(3)]
    return pull + [weight * w[c] for c in range(3)] + [radial * pull[c] for c in range(3)]


def force_kernel(nbr, star_total, row_ref, part_ref, old_ref, near_ref, far_ref,
                 reg_ref, irr_ref, new_ref, columns, fetched, picked, home, totals):
    active = row_ref.shape[0]
    entries = nbr + 1
    held, _, local = near_ref.shape
    tiles = local // LANES
    shards = BLOCK // tiles
    blocks = 2 * held // shards
    groups = active // SUB
    share = blocks // SUB

    def tile(block, s):
        ref, base = (near_ref, 0) if block < blocks // 2 else (far_ref, blocks // 2)
        p = (block - base) * shards + s // tiles
        return ref.at[p, :, pl.ds((s % tiles) * LANES, LANES)]

    for b in range(blocks):
        stacked = jnp.concatenate([tile(b, s)[...] for s in range(BLOCK)], axis=0)
        columns[b * LANES:(b + 1) * LANES, :] = stacked.T

    for i in range(active):
        fetched[i:i + 1, :] = columns[pl.ds(row_ref[i, 0], 1), :]
    for g in range(groups):
        rows = slice(g * SUB, (g + 1) * SUB)
        raw = fetched[rows, :]
        first = jnp.broadcast_to(part_ref[rows, 0:1], (SUB, LANES)) * SUB
        for c in range(6):
            home[c, rows, :] = jnp.take_along_axis(raw, first + c, axis=1, mode="promise_in_bounds")

    zero = jnp.zeros((SUB, LANES), jnp.float32)
    totals[...] = jnp.zeros(totals.shape, jnp.float32)

    def select(i):
        base = pl.multiple_of((i & 1) * LANES, LANES)
        turned = fetched[pl.ds(base, LANES), :].T
        part = jnp.broadcast_to(part_ref[pl.ds(i, 1), :], (SUB, LANES))
        kept = zero
        for s in range(BLOCK):
            kept = jnp.where(part == s, turned[s * SUB:(s + 1) * SUB, :], kept)
        picked[pl.ds(pl.multiple_of(i * SUB, SUB), SUB), :] = kept

    def fetch(i):
        base = (i & 1) * LANES
        for k in range(entries):
            fetched[pl.ds(base + k, 1), :] = columns[pl.ds(row_ref[i, k], 1), :]

    def sweep(i):
        rows = pl.ds(pl.multiple_of((i // SUB) * SUB, SUB), SUB)
        xi = [home[c, rows, :] for c in range(6)]
        sums = [zero] * 9
        for j in range(share):
            for half, ref in ((0, near_ref), (1, far_ref)):
                for q in range(shards // 2):
                    p = (lax.rem(i, SUB) * share + j) * (shards // 2) + q
                    for t in range(tiles):
                        xj = [jnp.broadcast_to(ref[p, c:c + 1, t * LANES:(t + 1) * LANES], (SUB, LANES)) for c in range(7)]
                        sums = [a + b for a, b in zip(sums, pair(xi, xj))]
        for c in range(3):
            totals[c, rows, :] += sums[c]
            totals[c + 3, rows, :] += sums[c + 3] - 3.0 * sums[c + 6]

    fetch(0)

    def step(i, _):
        select(i - 1)
        fetch(i)
        sweep(i)
        return 0

    sweep(0)
    lax.fori_loop(1, active, step, 0)
    select(active - 1)

    regular = [jnp.sum(totals[c].T, axis=0, keepdims=True) * (1.0 / star_total) for c in range(6)]
    for g in range(groups):
        rows = slice(g * SUB, (g + 1) * SUB)
        xj = [picked[pl.ds(g * SUB * SUB + c, SUB, stride=SUB), :] for c in range(7)]
        got = pair([home[c, rows, :] for c in range(6)], xj)
        for c in range(3):
            totals[c, rows, :] = got[c]
            totals[c + 3, rows, :] = got[c + 3] - 3.0 * got[c + 6]
    irregular = [jnp.sum(totals[c].T, axis=0, keepdims=True) * (1.0 / nbr) for c in range(6)]
    own = [home[c].T[0:1, :] for c in range(6)]
    for c in range(6):
        reg_ref[c:c + 1, :] = regular[c]
        irr_ref[c:c + 1, :] = irregular[c]
    for c in range(3):
        accel = regular[c] + irregular[c]
        jerk = regular[c + 3] + irregular[c + 3]
        a0, j0 = old_ref[c:c + 1, :], old_ref[c + 3:c + 4, :]
        difference = a0 - accel
        snap = -6.0 * difference - step_length * (4.0 * j0 + 2.0 * jerk)
        crackle = 12.0 * difference + 6.0 * step_length * (j0 + jerk)
        square = step_length * step_length
        new_ref[c:c + 1, :] = own[c] + square / 24.0 * snap + square / 120.0 * crackle
        new_ref[c + 3:c + 4, :] = own[c + 3] + step_length / 6.0 * snap + step_length / 24.0 * crackle


def per_device(field_phase, field_mass, old_force, target_slot, target_star):
    entries, active = target_slot.shape
    count = lax.axis_size("grp") * lax.axis_size("blk")
    local = field_phase.shape[1]
    nbr = entries - 1
    bucket = 2 * ((entries * active + count - 1) // count)
    tiles = local // LANES
    assert count & (count - 1) == 0 and active % SUB == 0 and entries <= LANES
    assert local % LANES == 0 and BLOCK % (2 * tiles) == 0 and (count * tiles) % (BLOCK * SUB) == 0
    me = lax.axis_index("grp") * lax.axis_size("blk") + lax.axis_index("blk")
    bits = [1 << b for b in reversed(range(count.bit_length() - 1))]

    slot = jnp.pad(target_slot.T, ((0, 0), (0, LANES - entries)))
    star = jnp.pad(target_star.T, ((0, 0), (0, LANES - entries)))
    rel = (slot // bucket) ^ me
    pos = sum(((rel >> (bit.bit_length() - 1)) & 1) << weight for weight, bit in enumerate(bits))
    where = pos * tiles + star // LANES
    row = where // BLOCK * LANES + star % LANES
    part = jnp.where(jnp.arange(LANES)[None, :] < entries, where % BLOCK, -1)

    table = jnp.concatenate([field_phase, field_mass[None, :], jnp.zeros((1, local), jnp.float32)], axis=0)[None]
    for bit in bits[:-1]:
        table = jnp.concatenate([table, swapped(table, bit, count)], axis=0)
    other = swapped(table, bits[-1], count)
    table, other = (pltpu.with_memory_space_constraint(x, pltpu.VMEM) for x in (table, other))
    vmem = pl.BlockSpec(memory_space=pltpu.VMEM)
    out = jax.ShapeDtypeStruct((6, active), jnp.float32)
    f32 = jnp.float32
    return pl.pallas_call(
        functools.partial(force_kernel, nbr, local * count),
        out_shape=(out, out, out),
        in_specs=[pl.BlockSpec(memory_space=pltpu.SMEM)] + [vmem] * 4,
        out_specs=(vmem, vmem, vmem),
        scratch_shapes=[
            pltpu.VMEM((count * tiles // BLOCK * LANES, LANES), f32),
            pltpu.VMEM((2 * LANES, LANES), f32),
            pltpu.VMEM((active * SUB, LANES), f32),
            pltpu.VMEM((6, active, LANES), f32),
            pltpu.VMEM((6, active, LANES), f32),
        ],
        compiler_params=pltpu.CompilerParams(vmem_limit_bytes=32 << 20),
        name="forces",
    )(row, part, old_force, table, other)


def solution(mesh):
    spec = P(None, AXES)
    return jax.shard_map(
        per_device, mesh=mesh, in_specs=(spec, P(AXES), spec, spec, spec),
        out_specs=(spec, spec, spec), check_vma=False,
    )
```

```python
import functools

import jax
import jax.numpy as jnp
from jax import lax
from jax.experimental import pallas as pl
from jax.experimental.pallas import tpu as pltpu
from jax.sharding import PartitionSpec as P

soften_sq = 0.01
step_length = 0.5
AXES = ("grp", "blk")
LANES = 128
SUB = 8
BLOCK = LANES // SUB


def swapped(x, bit, count):
    return lax.ppermute(x, AXES, [(i, i ^ bit) for i in range(count)])


def pack_kernel(phase_ref, mass_ref, out_ref):
    out_ref[0, 0:6, :] = phase_ref[...]
    out_ref[0, 6:7, :] = mass_ref[...]
    out_ref[0, 7:8, :] = jnp.zeros((1, out_ref.shape[2]), jnp.float32)


def place_kernel(own_ref, row_ref, own_out, warm_out, sems):
    copies = [
        pltpu.make_async_copy(own_ref, own_out, sems.at[0]),
        pltpu.make_async_copy(row_ref.at[0:warm_out.shape[0], :], warm_out, sems.at[1]),
    ]
    for copy in copies:
        copy.start()
    for copy in copies:
        copy.wait()


def placed(own, row, warm):
    vmem, smem = (pl.BlockSpec(memory_space=space) for space in (pltpu.VMEM, pltpu.SMEM))
    return pl.pallas_call(
        place_kernel,
        out_shape=(pltpu.SMEM(own.shape, own.dtype), pltpu.SMEM((warm, row.shape[1]), row.dtype)),
        in_specs=[vmem, vmem],
        out_specs=(smem, smem),
        scratch_shapes=[pltpu.SemaphoreType.DMA((2,))],
        name="place",
    )(*(pltpu.with_memory_space_constraint(x, pltpu.VMEM) for x in (own, row)))


def spread(table, high, low, count):
    got = {}
    for part, bit in (("both", high | low), ("low", low), ("high", high)):
        got[part] = swapped(table, bit, count)
    return jnp.concatenate([table, got["high"], got["low"], got["both"]], axis=0)


def packed(phase, mass):
    local = phase.shape[1]
    vmem = pl.BlockSpec(memory_space=pltpu.VMEM)
    return pl.pallas_call(
        pack_kernel,
        out_shape=pltpu.VMEM((1, 8, local), jnp.float32),
        in_specs=[vmem, vmem],
        out_specs=pl.BlockSpec(memory_space=pltpu.VMEM),
        name="pack",
    )(phase, mass[None, :])


def pair(xi, xj):
    d = [xj[c] - xi[c] for c in range(3)]
    w = [xj[c + 3] - xi[c + 3] for c in range(3)]
    dist_sq = soften_sq + (d[0] * d[0] + d[1] * d[1] + d[2] * d[2])
    inverse = lax.rsqrt(dist_sq)
    inv_sq = inverse * inverse
    weight = (xj[6] * inverse) * inv_sq
    radial = (d[0] * w[0] + d[1] * w[1] + d[2] * w[2]) * inv_sq
    pull = [weight * d[c] for c in range(3)]
    return pull + [weight * w[c] for c in range(3)] + [radial * pull[c] for c in range(3)]


def force_kernel(nbr, star_total, own_ref, warm_ref, rows_ref, part_ref, old_hbm, near_ref, far_ref,
                 reg_ref, irr_ref, new_ref, row_ref, columns, fetched, picked, home, totals, old_ref, sem, old_sem):
    active = part_ref.shape[0]
    warm = warm_ref.shape[0]
    entries = nbr + 1
    held, _, local = near_ref.shape
    tiles = local // LANES
    shards = BLOCK // tiles
    blocks = 2 * held // shards
    groups = active // SUB
    share = blocks // SUB

    def tile(block, s):
        ref, base = (near_ref, 0) if block < blocks // 2 else (far_ref, blocks // 2)
        p = (block - base) * shards + s // tiles
        return ref.at[p, :, pl.ds((s % tiles) * LANES, LANES)]

    filling = pltpu.make_async_copy(rows_ref, row_ref, sem)
    filling.start()
    fetching = pltpu.make_async_copy(old_hbm, old_ref, old_sem)
    fetching.start()

    for b in range(blocks):
        stacked = jnp.concatenate([tile(b, s)[...] for s in range(BLOCK)], axis=0)
        columns[b * LANES:(b + 1) * LANES, :] = stacked.T

    fetched[...] = jnp.zeros(fetched.shape, jnp.float32)

    for i in range(active):
        totals[0, i:i + 1, :] = columns[pl.ds(own_ref[i], 1), :]
    for g in range(groups):
        rows = slice(g * SUB, (g + 1) * SUB)
        raw = totals[0, rows, :]
        first = jnp.broadcast_to(part_ref[rows, 0:1], (SUB, LANES)) * SUB
        for c in range(6):
            home[c, rows, :] = jnp.take_along_axis(raw, first + c, axis=1, mode="promise_in_bounds")

    zero = jnp.zeros((SUB, LANES), jnp.float32)
    totals[...] = jnp.zeros(totals.shape, jnp.float32)

    def turn(odd):
        return fetched[pl.ds(pl.multiple_of(odd * LANES, LANES), LANES), :].T

    def keep(i, turned):
        part = jnp.broadcast_to(part_ref[pl.ds(i, 1), :], (SUB, LANES))
        left = [turned[s * SUB:(s + 1) * SUB, :] for s in range(BLOCK)]
        bit = 1
        while len(left) > 1:
            odd = (part & bit) != 0
            left = [jnp.where(odd, left[n + 1], left[n]) for n in range(0, len(left), 2)]
            bit *= 2
        return left[0]

    def put(i, kept):
        picked[pl.ds(pl.multiple_of(i * SUB, SUB), SUB), :] = kept

    def fetch(source, i, odd):
        slot = fetched.at[pl.ds(pl.multiple_of(odd * LANES, LANES), LANES), :]
        for k in range(1, entries):
            slot[k:k + 1, :] = columns[pl.ds(source.at[:, pl.ds(k, 1)][i, 0], 1), :]

    def sweep(source, i, odd, before):
        rows = pl.ds(pl.multiple_of((i // SUB) * SUB, SUB), SUB)
        xi = [home[c, rows, :] for c in range(6)]
        turned = turn(1 - odd)
        sums = [zero] * 9
        units = [(j, ref, q, t) for j in range(share) for ref in (near_ref, far_ref)
                 for q in range(shards // 2) for t in range(tiles)]
        for j, ref, q, t in units:
            p = (lax.rem(i, SUB) * share + j) * (shards // 2) + q
            xj = [jnp.broadcast_to(ref[p, c:c + 1, t * LANES:(t + 1) * LANES], (SUB, LANES)) for c in range(7)]
            sums = [a + b for a, b in zip(sums, pair(xi, xj))]
        put(before, keep(before, turned))
        fetch(source, i, odd)
        for c in range(3):
            totals[c, rows, :] += sums[c]
            totals[c + 3, rows, :] += sums[c + 3] - 3.0 * sums[c + 6]

    def step(source, i, _):
        sweep(source, i, i & 1, jnp.maximum(i - 1, 0))
        return 0

    lax.fori_loop(0, warm, functools.partial(step, warm_ref), 0)
    filling.wait()
    lax.fori_loop(warm, active, functools.partial(step, row_ref), 0, unroll=2)
    put(active - 1, keep(active - 1, turn((active - 1) & 1)))

    lanes = lax.broadcasted_iota(jnp.int32, (SUB, LANES), 1)
    results = []
    for g in range(groups):
        rows = slice(g * SUB, (g + 1) * SUB)
        xi = [home[c, rows, :] for c in range(6)]
        xj = [picked[pl.ds(g * SUB * SUB + c, SUB, stride=SUB), :] for c in range(7)]
        got = pair(xi, xj)
        near = [got[c] for c in range(3)] + [got[c + 3] - 3.0 * got[c + 6] for c in range(3)]
        values = [jnp.sum(totals[c, rows, :], axis=1, keepdims=True) for c in range(6)]
        values += [jnp.sum(v, axis=1, keepdims=True) for v in near]
        result = zero
        for n, v in enumerate(values + xi):
            result = jnp.where(lanes == n, jnp.broadcast_to(v, (SUB, LANES)), result)
        results.append(result)
    results = jnp.concatenate(results, axis=0).T
    regular = [results[c:c + 1, :] * (1.0 / star_total) for c in range(6)]
    irregular = [results[c + 6:c + 7, :] * (1.0 / nbr) for c in range(6)]
    own = [results[c + 12:c + 13, :] for c in range(6)]
    fetching.wait()
    for c in range(6):
        reg_ref[c:c + 1, :] = regular[c]
        irr_ref[c:c + 1, :] = irregular[c]
    for c in range(3):
        accel = regular[c] + irregular[c]
        jerk = regular[c + 3] + irregular[c + 3]
        a0, j0 = old_ref[c:c + 1, :], old_ref[c + 3:c + 4, :]
        difference = a0 - accel
        snap = -6.0 * difference - step_length * (4.0 * j0 + 2.0 * jerk)
        crackle = 12.0 * difference + 6.0 * step_length * (j0 + jerk)
        square = step_length * step_length
        new_ref[c:c + 1, :] = own[c] + square / 24.0 * snap + square / 120.0 * crackle
        new_ref[c + 3:c + 4, :] = own[c + 3] + step_length / 6.0 * snap + step_length / 24.0 * crackle


def per_device(field_phase, field_mass, old_force, target_slot, target_star):
    entries, active = target_slot.shape
    count = lax.axis_size("grp") * lax.axis_size("blk")
    local = field_phase.shape[1]
    nbr = entries - 1
    bucket = 2 * ((entries * active + count - 1) // count)
    tiles = local // LANES
    assert count & (count - 1) == 0 and active % SUB == 0 and entries <= LANES
    assert local % LANES == 0 and BLOCK % (2 * tiles) == 0 and (count * tiles) % (BLOCK * SUB) == 0
    me = lax.axis_index("grp") * lax.axis_size("blk") + lax.axis_index("blk")
    bits = [1 << b for b in reversed(range(count.bit_length() - 1))]

    slot = jnp.pad(target_slot.T, ((0, 0), (0, LANES - entries)))
    star = jnp.pad(target_star.T, ((0, 0), (0, LANES - entries)))
    rel = (slot // bucket) ^ me
    pos = sum(((rel >> (bit.bit_length() - 1)) & 1) << weight for weight, bit in enumerate(bits))
    where = pos * tiles + star // LANES
    row = where // BLOCK * LANES + star % LANES
    part = where % BLOCK

    own, warm = placed(row[:, 0], row, SUB)
    table = packed(field_phase, field_mass)
    for bit in bits[:-5]:
        table = jnp.concatenate([table, swapped(table, bit, count)], axis=0)
    table = spread(table, bits[-5], bits[-4], count)
    table = spread(table, bits[-3], bits[-2], count)
    other = swapped(table, bits[-1], count)
    row, table, other = (pltpu.with_memory_space_constraint(x, pltpu.VMEM) for x in (row, table, other))
    vmem = pl.BlockSpec(memory_space=pltpu.VMEM)
    out = jax.ShapeDtypeStruct((6, active), jnp.float32)
    f32 = jnp.float32
    return pl.pallas_call(
        functools.partial(force_kernel, nbr, local * count),
        out_shape=(out, out, out),
        in_specs=[pl.BlockSpec(memory_space=pltpu.SMEM)] * 2 + [vmem] * 2 + [pl.BlockSpec(memory_space=pl.ANY)] + [vmem] * 2,
        out_specs=(vmem, vmem, vmem),
        scratch_shapes=[
            pltpu.SMEM(part.shape, jnp.int32),
            pltpu.VMEM((count * tiles // BLOCK * LANES, LANES), f32),
            pltpu.VMEM((2 * LANES, LANES), f32),
            pltpu.VMEM((active * SUB, LANES), f32),
            pltpu.VMEM((6, active, LANES), f32),
            pltpu.VMEM((6, active, LANES), f32),
            pltpu.VMEM((6, active), f32),
            pltpu.SemaphoreType.DMA,
            pltpu.SemaphoreType.DMA,
        ],
        compiler_params=pltpu.CompilerParams(vmem_limit_bytes=32 << 20),
        name="forces",
    )(own, warm, row, part, pltpu.with_memory_space_constraint(old_force, pltpu.MemorySpace.HBM), table, other)


def solution(mesh):
    spec = P(None, AXES)
    return jax.shard_map(
        per_device, mesh=mesh, in_specs=(spec, P(AXES), spec, spec, spec),
        out_specs=(spec, spec, spec), check_vma=False,
    )
```
